32 devices in a mesh: egrp: 2 (over x), space: 16 (over z, y, core).
Axes of the slice: x: 2, y: 2, z: 4, core: 2. Of those that a mesh axis runs over, the one named last changes fastest.
Arguments:
- dist: float32 [2, 1024, 64, 128], P(None, 'egrp', 'space'), may hold values from -12 to 12
- hist_x: bfloat16 [4, 2, 1024, 64, 128], P(None, None, 'egrp', 'space'), may hold values from -6 to 6
- hist_g: bfloat16 [4, 2, 1024, 64, 128], P(None, None, 'egrp', 'space'), may hold values from -12 to 12
- mobility: float32 [64, 128], P('space'), may hold values from 0.2 to 2
- region: int32 [64, 128], P('space'), may hold values from 0 to 3
- phonon_bins: int32 [4], replicated, may hold values from 48 to 64, as said below
- coupling: float32 [4], replicated, may hold values from 0.2 to 1.5
- hist_used: int32 [2, 4], replicated, may hold values 0 or 1
Outputs:
- drifted: float32 [2, 1024, 64, 128], P(None, 'egrp', 'space')
The draws below stay inside these ranges and needn't reach their ends.
Inputs may be any that keep to these rules, and one draw needn't show every extreme that they name: `phonon_bins`: each value lies in 48 to 64; both ends occur.
All inputs are finite; a program needn't handle non-finite values.
Results may differ from the reference program's by a relative error of at most 0.0003.
Values sent between devices are 32-bit elements; how exact they have to be, the bound alone decides.
A program may use at most 128 MiB of HBM per device.

```python
import math
import jax
import jax.numpy as jnp
from jax import lax

NE = 1024
HISTORY = 4
NREGION = 4
KMIN = 48
KMAX = 64
COLS = 64
NZC = 128
NROWS = 64


def draw_phonon_bins(key, part):
    values = jax.random.randint(key, (NREGION,), KMIN, KMAX + 1)
    first = jax.random.randint(jax.random.fold_in(key, 1), (), 0, NREGION)
    second = (first + 1 + jax.random.randint(jax.random.fold_in(key, 2), (), 0, NREGION - 1)) % NREGION
    values = values.at[first].set(KMAX)
    values = values.at[second].set(KMIN)
    return values.astype(jnp.int32)


def shared_field(key):
    shape = (2, NE, NROWS, NZC)
    energy_level = jnp.exp(jax.random.uniform(jax.random.fold_in(key, 11), (1, NE, 1, 1), jnp.float32, jnp.log(0.5), jnp.log(2.0)))
    row_level = jnp.exp(jax.random.uniform(jax.random.fold_in(key, 12), (1, 1, NROWS, 1), jnp.float32, jnp.log(0.5), jnp.log(2.0)))
    levels = energy_level * row_level
    base = jnp.clip(jax.random.normal(jax.random.fold_in(key, 13), shape, jnp.float32), -3.0, 3.0)
    return (levels, base)


def draw_dist(key, part):
    levels, base = shared_field(key)
    return jnp.clip(levels * base, -12.0, 12.0).astype(jnp.float32)


def draw_hist_g(key, part):
    levels, base = shared_field(key)
    shape = (HISTORY, 2, NE, NROWS, NZC)
    along = jnp.exp(jax.random.uniform(jax.random.fold_in(key, 3), (HISTORY, 1, 1, 1, 1), jnp.float32, jnp.log(0.2), jnp.log(0.8)))
    spread = jnp.exp(jax.random.uniform(jax.random.fold_in(key, 7), (HISTORY, 1, 1, 1, 1), jnp.float32, jnp.log(0.5), jnp.log(1.5)))
    noise = jnp.clip(jax.random.normal(jax.random.fold_in(key, 6), shape, jnp.float32), -3.0, 3.0)
    values = levels[None] * (spread * noise - along * base[None])
    return jnp.clip(values, -12.0, 12.0).astype(jnp.bfloat16)


def place_ends(values, key, least, top_value):
    longest = values.shape.index(max(values.shape))
    spots = []
    for shift in (0, 1):
        where = [jax.random.randint(jax.random.fold_in(key, axis), (), 0, length) for axis, length in enumerate(values.shape)]
        where[longest] = (where[longest] + shift) % values.shape[longest]
        spots.append(tuple(where))
    return values.at[spots[0]].set(least).at[spots[1]].set(top_value)


def level_of(rng, dims, shards, low, top_value):
    level, own = 1.0, jax.random.fold_in(rng, 6)
    for position, shards_of in shards:
        steps = jnp.exp(jax.random.uniform(jax.random.fold_in(own, position), (shards_of,), jnp.float32, low / len(shards), top_value / len(shards)))
        level = level * jnp.repeat(steps, dims[position] // shards_of).reshape([-1 if axis == position else 1 for axis in range(len(dims))])
    return level


def centred(key, shape, scale, bound, split=(), held_as=jnp.bfloat16):
    entries = jax.random.normal(key, shape, jnp.float32) * scale
    if len(split) > 0:
        entries = level_of(key, shape, split, -0.22, 0.18) * entries
    return jnp.clip(entries, min=-bound, max=bound).astype(held_as)


def setup_inputs(seed: int = 0) -> dict:
    splits = jax.random.split(jax.random.key(seed), 9)
    return {
        "dist": draw_dist(jax.random.fold_in(splits[8], 71), 0),
        "hist_x": centred(splits[1], (HISTORY, 2, NE, NROWS, NZC), 1.0, 6.0, ((2, 2), (3, 16))),
        "hist_g": draw_hist_g(jax.random.fold_in(splits[8], 71), 0),
        "mobility": jnp.clip(jnp.exp(math.log(2.0) - 2.3025851 * jax.random.uniform(splits[3], (NROWS, NZC), jnp.float32) ** level_of(splits[3], (NROWS, NZC), ((0, 16),), -0.2, 0.2)), 0.2, 2.0),
        "region": place_ends(jax.random.randint(splits[4], (NROWS, NZC), 0, NREGION), jax.random.fold_in(splits[4], 1), 0, NREGION - 1).astype(jnp.int32),
        "phonon_bins": draw_phonon_bins(jax.random.fold_in(splits[8], 71), 0),
        "coupling": jnp.clip(jnp.exp(jax.random.uniform(splits[6], (NREGION,), jnp.float32, math.log(0.2), math.log(1.5))), 0.2, 1.5),
        "hist_used": place_ends((jax.random.randint(splits[7], (2, HISTORY), 0, 2) < 1).astype(jnp.int32), jax.random.fold_in(splits[7], 1), 0, 1),
    }


def neighbour_sum(field, mobility):
    total = jnp.zeros(field.shape, jnp.float32)
    rows = field.shape[2]
    cells = field.shape[3]
    row_ids = jnp.arange(rows, dtype=jnp.int32)[:, None]
    cell_ids = jnp.arange(cells, dtype=jnp.int32)[None, :]
    column = cell_ids % COLS
    for shift_by, axis, valid in ((1, 0, row_ids > 0), (-1, 0, row_ids < rows - 1), (1, 1, column > 0), (-1, 1, column < COLS - 1), (COLS, 1, cell_ids >= COLS), (-COLS, 1, cell_ids < COLS)):
        moved = jnp.roll(field, shift_by, axis=axis + 2)
        moved_mob = jnp.roll(mobility, shift_by, axis=axis)
        flux = 0.5 * (mobility + moved_mob)
        total = total + jnp.where(valid, flux * (moved - field), 0.0)
    return total

def reference(dist, hist_x, hist_g, mobility, region, phonon_bins, coupling, hist_used):
    even = dist[0]
    odd = dist[1]
    energy_ids = jnp.arange(NE, dtype=jnp.int32)
    dos = jnp.sqrt((energy_ids.astype(jnp.float32) + 0.5) / NE)
    padded = jnp.pad(even, ((KMAX, KMAX), (0, 0), (0, 0)))
    shifted = jnp.zeros(even.shape, jnp.float32)
    outrate = jnp.zeros(even.shape, jnp.float32)
    lam = jnp.zeros(region.shape, jnp.float32)
    for index in range(NREGION):
        offset = phonon_bins[index].astype(jnp.int32)
        above = lax.dynamic_slice_in_dim(padded, (KMAX + offset).astype(jnp.int32), NE, 0)
        below = lax.dynamic_slice_in_dim(padded, (KMAX - offset).astype(jnp.int32), NE, 0)
        lower = energy_ids - offset
        upper = energy_ids + offset
        dos_low = jnp.where(lower >= 0, jnp.sqrt((jnp.maximum(lower, 0).astype(jnp.float32) + 0.5) / NE), 0.0)
        dos_high = jnp.where(upper < NE, jnp.sqrt((upper.astype(jnp.float32) + 0.5) / NE), 0.0)
        rate = coupling[index] * (1.5 * dos_low + 0.5 * dos_high)
        inside = (region == index)[None]
        shifted = jnp.where(inside, 1.5 * above + 0.5 * below, shifted)
        outrate = jnp.where(inside, rate[:, None, None], outrate)
        lam = jnp.where(region == index, coupling[index], lam)
    gain_in = lam[None] * dos[:, None, None] * shifted
    new_even = (even + gain_in) / (1.0 + outrate)
    new_odd = odd / (1.0 + outrate + lam[None])
    res = jnp.stack([new_even - even, new_odd - odd])
    fields = []
    for field in range(2):
        vectors = [res[field]] + [hist_g[index, field].astype(jnp.float32) for index in range(HISTORY)]
        gram = jnp.zeros((HISTORY + 1, HISTORY + 1), jnp.float32)
        for left in range(HISTORY + 1):
            for right in range(HISTORY + 1):
                gram = gram.at[left, right].set(jnp.sum(vectors[left] * vectors[right]))
        valid = jnp.concatenate([jnp.ones((1,), jnp.float32), hist_used[field].astype(jnp.float32)])
        masked = valid[:, None] * valid[None, :] * gram + jnp.diag(1.0 - valid) * gram[0, 0]
        factor = jnp.linalg.cholesky(masked)
        weights = jax.scipy.linalg.cho_solve((factor, True), valid)
        coeffs = weights / jnp.sum(weights)
        part_mix = coeffs[0] * (dist[field] + 0.5 * res[field])
        for index in range(HISTORY):
            part_mix = part_mix + coeffs[index + 1] * (hist_x[index, field].astype(jnp.float32) + 0.5 * hist_g[index, field].astype(jnp.float32))
        fields.append(part_mix)
    mixed = jnp.stack(fields)
    lap = neighbour_sum(mixed, mobility)
    drive = 0.25 * dos[:, None, None]
    out_even = mixed[0] + 0.08 * lap[0] + drive * mixed[1]
    out_odd = mixed[1] + 0.08 * lap[1] - drive * mixed[0]
    return jnp.stack([out_even, out_odd])
```

```python
import functools
import jax
import jax.numpy as jnp
from jax import lax
from jax.experimental import pallas as pl
from jax.experimental.pallas import tpu as pltpu
from jax.sharding import PartitionSpec as P

NE = 1024
HISTORY = 4
NREGION = 4
KMAX = 64
COLS = 64
PIECES = 4
STEP = 16
PAIRS = [(i, j) for i in range(HISTORY + 1) for j in range(i, HISTORY + 1)]
MESH = pl.DeviceIdType.MESH


def dos_of(energy):
    return jnp.sqrt((energy.astype(jnp.float32) + 0.5) * (1.0 / NE))


def solve(total, field, used_ref):
    def entry(i, j):
        lane = field * len(PAIRS) + PAIRS.index((min(i, j), max(i, j)))
        return jnp.broadcast_to(total[:, lane : lane + 1], (8, 128))

    size = HISTORY + 1
    valid = [jnp.ones((8, 128), jnp.float32)]
    for index in range(HISTORY):
        valid.append(jnp.full((8, 128), used_ref[field, index].astype(jnp.float32)))
    first = entry(0, 0)
    low = [[None] * size for _ in range(size)]
    scaled = [[None] * size for _ in range(size)]
    inverse = [None] * size
    for j in range(size):
        for i in range(j, size):
            value = valid[i] * valid[j] * entry(i, j)
            if i == j:
                value = value + (1.0 - valid[i]) * first
            for k in range(j):
                value = value - scaled[i][k] * low[j][k]
            scaled[i][j] = value
        inverse[j] = 1.0 / scaled[j][j]
        for i in range(j + 1, size):
            low[i][j] = scaled[i][j] * inverse[j]
    forward = []
    for i in range(size):
        value = valid[i]
        for k in range(i):
            value = value - low[i][k] * forward[k]
        forward.append(value)
    weights = [None] * size
    for i in reversed(range(size)):
        value = forward[i] * inverse[i]
        for k in range(i + 1, size):
            value = value - low[k][i] * weights[k]
        weights[i] = value
    inv_sum = 1.0 / functools.reduce(lambda a, b: a + b, weights)
    return [w * inv_sum for w in weights]


def kernel(
    n_egrp, n_space, ne, rows,
    bins_ref, coup_ref, used_ref, mob_ref, region_ref, dist_hbm, hx_hbm, hg_hbm,
    out_hbm,
    even, odd, hg, hx, base, hist, mixed, out, lo, hi, offs, lam_ref, tile, weight,
    mob_send, mob_lo, mob_hi, sums, part, gathered, halo,
    in_sem, out_sem, halo_send, halo_recv, mob_ssem, mob_rsem, sum_send, sum_recv,
    edge_send, edge_recv,
):
    my_e = lax.axis_index("egrp")
    my_s = lax.axis_index("space")
    count = n_egrp * n_space
    me = my_e * n_space + my_s
    total_rows = ne * rows
    pad = KMAX * rows

    def device(index):
        return (index // n_space, lax.rem(index, n_space))

    loads = [
        pltpu.make_async_copy(dist_hbm.at[0], even.at[pl.ds(pad, total_rows)], in_sem.at[0]),
        pltpu.make_async_copy(dist_hbm.at[1], odd, in_sem.at[1]),
    ]
    for index in range(HISTORY):
        loads.append(pltpu.make_async_copy(hg_hbm.at[index], hg.at[index], in_sem.at[2 + index]))
    late = [
        pltpu.make_async_copy(hx_hbm.at[index], hx.at[index], in_sem.at[2 + HISTORY + index])
        for index in range(HISTORY)
    ]
    for copy in loads + late:
        copy.start()

    barrier = pltpu.get_barrier_semaphore()

    def greet(step, carry):
        pl.semaphore_signal(
            barrier, inc=1, device_id=device(lax.rem(me + step, count)), device_id_type=MESH
        )
        return carry

    lax.fori_loop(1, count, greet, 0)

    for copy_of in range(STEP // rows):
        tile[pl.ds(copy_of * rows, rows), :] = region_ref[...]
    region = tile[...]
    inside = [region == index for index in range(NREGION)]
    bins = jnp.zeros((STEP, 128), jnp.int32)
    lam = jnp.zeros((STEP, 128), jnp.float32)
    for index in range(NREGION):
        bins = jnp.where(inside[index], bins_ref[index], bins)
        lam = jnp.where(inside[index], coup_ref[index], lam)
    offs[...] = bins
    lam_ref[...] = lam
    mob_send[0] = mob_ref[0:1, :]
    mob_send[1] = mob_ref[rows - 1 : rows, :]

    has_below_e = my_e > 0
    has_above_e = my_e < n_egrp - 1
    has_below = my_s > 0
    has_above = my_s < n_space - 1

    even[pl.ds(0, pad), :] = jnp.zeros((pad, 128), jnp.float32)
    even[pl.ds(pad + total_rows, pad), :] = jnp.zeros((pad, 128), jnp.float32)

    @pl.when(my_s == 0)
    def _():
        lo[...] = jnp.zeros(lo.shape, jnp.float32)
        mob_lo[...] = jnp.zeros(mob_lo.shape, jnp.float32)

    @pl.when(my_s == n_space - 1)
    def _():
        hi[...] = jnp.zeros(hi.shape, jnp.float32)
        mob_hi[...] = jnp.zeros(mob_hi.shape, jnp.float32)

    pl.semaphore_wait(barrier, count - 1)

    up_e = pltpu.make_async_remote_copy(
        dist_hbm.at[0, pl.ds(total_rows - pad, pad)], halo.at[0],
        halo_send.at[0], halo_recv.at[0],
        device_id=(lax.rem(my_e + 1, n_egrp), my_s), device_id_type=MESH,
    )
    down_e = pltpu.make_async_remote_copy(
        dist_hbm.at[0, pl.ds(0, pad)], halo.at[1],
        halo_send.at[1], halo_recv.at[1],
        device_id=(lax.rem(my_e + n_egrp - 1, n_egrp), my_s), device_id_type=MESH,
    )
    next_s = lax.rem(my_s + 1, n_space)
    prev_s = lax.rem(my_s + n_space - 1, n_space)
    up_mob = pltpu.make_async_remote_copy(
        mob_send.at[1], mob_lo, mob_ssem.at[0], mob_rsem.at[0],
        device_id=(my_e, next_s), device_id_type=MESH,
    )
    down_mob = pltpu.make_async_remote_copy(
        mob_send.at[0], mob_hi, mob_ssem.at[1], mob_rsem.at[1],
        device_id=(my_e, prev_s), device_id_type=MESH,
    )

    @pl.when(has_above_e)
    def _():
        up_e.start()

    @pl.when(has_below_e)
    def _():
        down_e.start()

    @pl.when(has_above)
    def _():
        up_mob.start()

    @pl.when(has_below)
    def _():
        down_mob.start()

    for copy in loads:
        copy.wait()

    def residuals(step, accs):
        row = pl.multiple_of(step * STEP, STEP)
        bins = offs[...]
        lam = lam_ref[...]
        energy = my_e * ne + (row + lax.broadcasted_iota(jnp.int32, (STEP, 128), 0)) // rows
        region = tile[...]
        above = None
        for index in range(NREGION):
            shift = bins_ref[index] * rows
            up = even[pl.ds(pad + row + shift, STEP), :]
            down = even[pl.ds(pad + row - shift, STEP), :]
            if above is None:
                above, below = up, down
            else:
                above = jnp.where(region == index, up, above)
                below = jnp.where(region == index, down, below)
        lower = energy - bins
        upper = energy + bins
        dos_low = jnp.where(lower >= 0, dos_of(jnp.maximum(lower, 0)), 0.0)
        dos_high = jnp.where(upper < NE, dos_of(upper), 0.0)
        loss = 1.0 + lam * (1.5 * dos_low + 0.5 * dos_high)
        own_even = even[pl.ds(pad + row, STEP), :]
        own_odd = odd[pl.ds(row, STEP), :]
        gain = lam * dos_of(energy) * (1.5 * above + 0.5 * below)
        res = [
            (own_even + gain) * (1.0 / loss) - own_even,
            own_odd * (1.0 / (loss + lam)) - own_odd,
        ]
        base[0, pl.ds(row, STEP), :] = own_even + 0.5 * res[0]
        base[1, pl.ds(row, STEP), :] = own_odd + 0.5 * res[1]
        new = []
        for field in range(2):
            vectors = [res[field]] + [
                hg[index, field, pl.ds(row, STEP), :].astype(jnp.float32)
                for index in range(HISTORY)
            ]
            for position, (i, j) in enumerate(PAIRS):
                product = vectors[i] * vectors[j]
                new.append(accs[field * len(PAIRS) + position] + (product[:8] + product[8:]))
        return tuple(new)

    accs = tuple(jnp.zeros((8, 128), jnp.float32) for _ in range(2 * len(PAIRS)))
    edge = pad // STEP
    steps = total_rows // STEP
    accs = lax.fori_loop(edge, steps - edge, residuals, accs)

    @pl.when(has_below_e)
    def _():
        up_e.wait_recv()
        even[pl.ds(0, pad), :] = halo[0]

    accs = lax.fori_loop(0, edge, residuals, accs)

    @pl.when(has_above_e)
    def _():
        down_e.wait_recv()
        even[pl.ds(pad + total_rows, pad), :] = halo[1]

    accs = lax.fori_loop(steps - edge, steps, residuals, accs)

    sums[...] = jnp.zeros(sums.shape, jnp.float32)
    for position, acc in enumerate(accs):
        sums[position : position + 1, :] = jnp.sum(acc, axis=0, keepdims=True)
    lane_sum = jnp.sum(sums[...], axis=1, keepdims=True)
    place = lax.broadcasted_iota(jnp.int32, sums.shape, 0) == lax.broadcasted_iota(
        jnp.int32, sums.shape, 1
    )
    row_sum = jnp.sum(jnp.where(place, lane_sum, 0.0), axis=0, keepdims=True)
    part[...] = row_sum
    gathered[me] = row_sum

    def send_sums(step, carry):
        pltpu.make_async_remote_copy(
            part, gathered.at[me], sum_send, sum_recv,
            device_id=device(lax.rem(me + step, count)), device_id_type=MESH,
        ).start()
        return carry

    lax.fori_loop(1, count, send_sums, 0)

    for copy in late:
        copy.wait()

    def join_history(step, carry):
        row = pl.multiple_of(step * STEP, STEP)
        for index in range(HISTORY):
            for field in range(2):
                hist[index, field, pl.ds(row, STEP), :] = hx[
                    index, field, pl.ds(row, STEP), :
                ].astype(jnp.float32) + 0.5 * hg[index, field, pl.ds(row, STEP), :].astype(
                    jnp.float32
                )
        return carry

    lax.fori_loop(0, steps, join_history, 0)

    @pl.when(has_below)
    def _():
        up_mob.wait_recv()

    @pl.when(has_above)
    def _():
        down_mob.wait_recv()

    lanes = lax.broadcasted_iota(jnp.int32, (1, 128), 1)
    column = lanes % COLS
    for row in range(rows):
        mob = mob_ref[row : row + 1, :]
        under = mob_lo[...] if row == 0 else mob_ref[row - 1 : row, :]
        over = mob_hi[...] if row == rows - 1 else mob_ref[row + 1 : row + 2, :]
        w_under = 0.04 * (mob + under)
        w_over = 0.04 * (mob + over)
        if row == 0:
            w_under = jnp.where(has_below, w_under, 0.0)
        if row == rows - 1:
            w_over = jnp.where(has_above, w_over, 0.0)
        w_left = jnp.where(column > 0, 0.04 * (mob + pltpu.roll(mob, 1, 1)), 0.0)
        w_right = jnp.where(column < COLS - 1, 0.04 * (mob + pltpu.roll(mob, 127, 1)), 0.0)
        w_plane = 0.04 * (mob + pltpu.roll(mob, COLS, 1))
        own = 1.0 - (w_under + w_over + w_left + w_right + w_plane)
        for place, value in enumerate((own, w_under, w_over, w_left, w_right, w_plane)):
            weight[row, place] = jnp.broadcast_to(value, (8, 128))

    sums_in = gathered.at[pl.ds(0, count - 1)]
    pltpu.make_async_copy(sums_in, sums_in, sum_recv).wait()
    total = jnp.sum(gathered[...], axis=0)
    coeffs = [solve(total, field, used_ref) for field in range(2)]

    piece = ne // PIECES
    groups = piece // 8

    def mix(which, start_group, stop_group):
        def body(group, carry):
            first = pl.multiple_of(group * 8, 8)
            for row in which:
                source = pl.ds(first * rows + row, 8, stride=rows)
                for field in range(2):
                    value = coeffs[field][0] * base[field, source, :]
                    for index in range(HISTORY):
                        value = value + coeffs[field][index + 1] * hist[index, field, source, :]
                    mixed[row, field, pl.ds(first, 8), :] = value
            return carry

        lax.fori_loop(start_group, stop_group, body, 0)

    sends = []
    for index in range(PIECES):
        mix((0, rows - 1), index * groups, (index + 1) * groups)
        span = pl.ds(index * piece, piece)
        up = pltpu.make_async_remote_copy(
            mixed.at[rows - 1, :, span], lo.at[:, span], edge_send.at[0, index],
            edge_recv.at[0, index], device_id=(my_e, next_s), device_id_type=MESH,
        )
        down = pltpu.make_async_remote_copy(
            mixed.at[0, :, span], hi.at[:, span], edge_send.at[1, index],
            edge_recv.at[1, index], device_id=(my_e, prev_s), device_id_type=MESH,
        )
        sends.append((up, down))

        @pl.when(has_above)
        def _():
            up.start()

        @pl.when(has_below)
        def _():
            down.start()

    def drift(which, start_group, stop_group):
        def body(group, carry):
            first = pl.multiple_of(group * 8, 8)
            span = pl.ds(first, 8)
            energy = my_e * ne + first + lax.broadcasted_iota(jnp.int32, (8, 128), 0)
            drive = 0.25 * dos_of(energy)
            for row in which:
                own = [mixed[row, field, span, :] for field in range(2)]
                for field in range(2):
                    value = own[field]
                    under = lo[field, span, :] if row == 0 else mixed[row - 1, field, span, :]
                    over = (
                        hi[field, span, :] if row == rows - 1 else mixed[row + 1, field, span, :]
                    )
                    result = (
                        weight[row, 0] * value
                        + weight[row, 1] * under
                        + weight[row, 2] * over
                        + weight[row, 3] * pltpu.roll(value, 1, 1)
                        + weight[row, 4] * pltpu.roll(value, 127, 1)
                        + weight[row, 5] * pltpu.roll(value, COLS, 1)
                    )
                    if field == 0:
                        result = result + drive * own[1]
                    else:
                        result = result - drive * own[0]
                    out[field, pl.ds(first * rows + row, 8, stride=rows), :] = result
            return carry

        lax.fori_loop(start_group, stop_group, body, 0)

    inner = tuple(range(1, rows - 1))
    if inner:
        mix(inner, 0, PIECES * groups)
        drift(inner, 0, PIECES * groups)

    stores = []
    for index in range(PIECES):
        up, down = sends[index]

        @pl.when(has_below)
        def _():
            up.wait_recv()

        @pl.when(has_above)
        def _():
            down.wait_recv()

        drift((0, rows - 1), index * groups, (index + 1) * groups)
        span = pl.ds(index * piece * rows, piece * rows)
        store = pltpu.make_async_copy(out.at[:, span], out_hbm.at[:, span], out_sem.at[index])
        store.start()
        stores.append(store)

    sums_out = gathered.at[pl.ds(0, count - 1)]
    pltpu.make_async_copy(sums_out, sums_out, sum_send).wait()

    @pl.when(has_above_e)
    def _():
        up_e.wait_send()

    @pl.when(has_below_e)
    def _():
        down_e.wait_send()

    @pl.when(has_above)
    def _():
        up_mob.wait_send()
        for up, _ in sends:
            up.wait_send()

    @pl.when(has_below)
    def _():
        down_mob.wait_send()
        for _, down in sends:
            down.wait_send()

    for store in stores:
        store.wait()


def local(n_egrp, n_space, dist, hist_x, hist_g, mobility, region, phonon_bins, coupling, hist_used):
    ne, rows = dist.shape[1], dist.shape[2]
    total = ne * rows
    pad = KMAX * rows
    count = n_egrp * n_space
    f32 = jnp.float32
    smem = pl.BlockSpec(memory_space=pltpu.SMEM)
    vmem = pl.BlockSpec(memory_space=pltpu.VMEM)
    hbm = pl.BlockSpec(memory_space=pl.ANY)
    result = pl.pallas_call(
        functools.partial(kernel, n_egrp, n_space, ne, rows),
        out_shape=jax.ShapeDtypeStruct((2, total, 128), f32),
        in_specs=[smem, smem, smem, vmem, vmem, hbm, hbm, hbm],
        out_specs=hbm,
        scratch_shapes=[
            pltpu.VMEM((total + 2 * pad, 128), f32),
            pltpu.VMEM((total, 128), f32),
            pltpu.VMEM((HISTORY, 2, total, 128), jnp.bfloat16),
            pltpu.VMEM((HISTORY, 2, total, 128), jnp.bfloat16),
            pltpu.VMEM((2, total, 128), f32),
            pltpu.VMEM((HISTORY, 2, total, 128), f32),
            pltpu.VMEM((rows, 2, ne, 128), f32),
            pltpu.VMEM((2, total, 128), f32),
            pltpu.VMEM((2, ne, 128), f32),
            pltpu.VMEM((2, ne, 128), f32),
            pltpu.VMEM((STEP, 128), jnp.int32),
            pltpu.VMEM((STEP, 128), f32),
            pltpu.VMEM((STEP, 128), jnp.int32),
            pltpu.VMEM((rows, 6, 8, 128), f32),
            pltpu.VMEM((2, 1, 128), f32),
            pltpu.VMEM((1, 128), f32),
            pltpu.VMEM((1, 128), f32),
            pltpu.VMEM((32, 128), f32),
            pltpu.VMEM((1, 128), f32),
            pltpu.VMEM((count, 1, 128), f32),
            pltpu.VMEM((2, pad, 128), f32),
            pltpu.SemaphoreType.DMA((2 + 2 * HISTORY,)),
            pltpu.SemaphoreType.DMA((PIECES,)),
            pltpu.SemaphoreType.DMA((2,)),
            pltpu.SemaphoreType.DMA((2,)),
            pltpu.SemaphoreType.DMA((2,)),
            pltpu.SemaphoreType.DMA((2,)),
            pltpu.SemaphoreType.DMA,
            pltpu.SemaphoreType.DMA,
            pltpu.SemaphoreType.DMA((2, PIECES)),
            pltpu.SemaphoreType.DMA((2, PIECES)),
        ],
        compiler_params=pltpu.CompilerParams(
            collective_id=0, has_side_effects=True, vmem_limit_bytes=48 << 20
        ),
    )(
        phonon_bins, coupling, hist_used, mobility, region,
        dist.reshape(2, total, 128),
        hist_x.reshape(HISTORY, 2, total, 128),
        hist_g.reshape(HISTORY, 2, total, 128),
    )
    return result.reshape(dist.shape)


def solution(mesh):
    in_specs = (
        P(None, "egrp", "space", None),
        P(None, None, "egrp", "space", None),
        P(None, None, "egrp", "space", None),
        P("space", None),
        P("space", None),
        P(),
        P(),
        P(),
    )
    out_specs = P(None, "egrp", "space", None)
    body = functools.partial(local, mesh.shape["egrp"], mesh.shape["space"])
    return jax.shard_map(body, mesh=mesh, in_specs=in_specs, out_specs=out_specs, check_vma=False)
```

```python
import functools
import jax
import jax.numpy as jnp
from jax import lax
from jax.experimental import pallas as pl
from jax.experimental.pallas import tpu as pltpu
from jax.sharding import PartitionSpec as P

NE = 1024
HISTORY = 4
NREGION = 4
KMAX = 64
COLS = 64
PIECES = 4
STEP = 16
WIDE = 32
PAIRS = [(i, j) for i in range(HISTORY + 1) for j in range(i, HISTORY + 1)]
MESH = pl.DeviceIdType.MESH


def dos_of(energy):
    return jnp.sqrt((energy.astype(jnp.float32) + 0.5) * (1.0 / NE))


def solve(total, field, used_ref):
    def entry(i, j):
        lane = field * len(PAIRS) + PAIRS.index((min(i, j), max(i, j)))
        return jnp.broadcast_to(total[:, lane : lane + 1], (8, 128))

    size = HISTORY + 1
    valid = [jnp.ones((8, 128), jnp.float32)]
    for index in range(HISTORY):
        valid.append(jnp.full((8, 128), used_ref[field, index].astype(jnp.float32)))
    first = entry(0, 0)
    low = [[None] * size for _ in range(size)]
    scaled = [[None] * size for _ in range(size)]
    inverse = [None] * size
    for j in range(size):
        for i in range(j, size):
            value = valid[i] * valid[j] * entry(i, j)
            if i == j:
                value = value + (1.0 - valid[i]) * first
            for k in range(j):
                value = value - scaled[i][k] * low[j][k]
            scaled[i][j] = value
        inverse[j] = 1.0 / scaled[j][j]
        for i in range(j + 1, size):
            low[i][j] = scaled[i][j] * inverse[j]
    forward = []
    for i in range(size):
        value = valid[i]
        for k in range(i):
            value = value - low[i][k] * forward[k]
        forward.append(value)
    weights = [None] * size
    for i in reversed(range(size)):
        value = forward[i] * inverse[i]
        for k in range(i + 1, size):
            value = value - low[k][i] * weights[k]
        weights[i] = value
    inv_sum = 1.0 / functools.reduce(lambda a, b: a + b, weights)
    return [w * inv_sum for w in weights]


def kernel(
    n_egrp, n_space, ne, rows,
    bins_hbm, coup_hbm, used_hbm, mob_hbm, region_hbm, dist_hbm, hx_hbm, hg_hbm,
    out,
    bins_ref, coup_ref, used_ref, mob_ref, region_ref,
    even, odd, hg, hx, base, hist, mixed, packed, lo, hi, offs, lam_ref, tile, weight,
    mob_send, mob_lo, mob_hi, sums, part, gathered, halo,
    in_sem, small_sem, halo_send, halo_recv, mob_ssem, mob_rsem, sum_send, sum_recv,
    edge_send, edge_recv,
):
    my_e = lax.axis_index("egrp")
    my_s = lax.axis_index("space")
    count = n_egrp * n_space
    me = my_e * n_space + my_s
    total_rows = ne * rows
    pad = KMAX * rows

    def device(index):
        return (index // n_space, lax.rem(index, n_space))

    small = [
        pltpu.make_async_copy(source, target, small_sem.at[index])
        for index, (source, target) in enumerate((
            (region_hbm, region_ref), (bins_hbm, bins_ref), (coup_hbm, coup_ref),
            (mob_hbm, mob_ref), (used_hbm, used_ref),
        ))
    ]
    loads = [
        pltpu.make_async_copy(dist_hbm.at[0], even.at[pl.ds(pad, total_rows)], in_sem.at[0]),
        pltpu.make_async_copy(dist_hbm.at[1], odd, in_sem.at[1]),
    ]
    for index in range(HISTORY):
        loads.append(pltpu.make_async_copy(hg_hbm.at[index], hg.at[index], in_sem.at[2 + index]))
    late = [
        pltpu.make_async_copy(hx_hbm.at[index], hx.at[index], in_sem.at[2 + HISTORY + index])
        for index in range(HISTORY)
    ]
    for copy in small + loads + late:
        copy.start()

    barrier = pltpu.get_barrier_semaphore()

    def greet(step, carry):
        pl.semaphore_signal(
            barrier, inc=1, device_id=device(lax.rem(me + step, count)), device_id_type=MESH
        )
        return carry

    lax.fori_loop(1, count, greet, 0)

    for copy in small:
        copy.wait()
    for copy_of in range(STEP // rows):
        tile[pl.ds(copy_of * rows, rows), :] = region_ref[...]
    region = tile[...]
    inside = [region == index for index in range(NREGION)]
    bins = jnp.zeros((STEP, 128), jnp.int32)
    lam = jnp.zeros((STEP, 128), jnp.float32)
    for index in range(NREGION):
        bins = jnp.where(inside[index], bins_ref[index], bins)
        lam = jnp.where(inside[index], coup_ref[index], lam)
    offs[...] = bins
    lam_ref[...] = lam
    mob_send[0] = mob_ref[0:1, :]
    mob_send[1] = mob_ref[rows - 1 : rows, :]

    has_below_e = my_e > 0
    has_above_e = my_e < n_egrp - 1
    has_below = my_s > 0
    has_above = my_s < n_space - 1

    for field in range(2):
        mixed[field, pl.ds(0, 8), :] = jnp.zeros((8, 128), jnp.float32)
        mixed[field, pl.ds(8 + total_rows, 8), :] = jnp.zeros((8, 128), jnp.float32)
    even[pl.ds(0, pad), :] = jnp.zeros((pad, 128), jnp.float32)
    even[pl.ds(pad + total_rows, pad), :] = jnp.zeros((pad, 128), jnp.float32)

    @pl.when(my_s == 0)
    def _():
        lo[...] = jnp.zeros(lo.shape, jnp.float32)
        mob_lo[...] = jnp.zeros(mob_lo.shape, jnp.float32)

    @pl.when(my_s == n_space - 1)
    def _():
        hi[...] = jnp.zeros(hi.shape, jnp.float32)
        mob_hi[...] = jnp.zeros(mob_hi.shape, jnp.float32)

    pl.semaphore_wait(barrier, count - 1)

    up_e = pltpu.make_async_remote_copy(
        dist_hbm.at[0, pl.ds(total_rows - pad, pad)], halo.at[0],
        halo_send.at[0], halo_recv.at[0],
        device_id=(lax.rem(my_e + 1, n_egrp), my_s), device_id_type=MESH,
    )
    down_e = pltpu.make_async_remote_copy(
        dist_hbm.at[0, pl.ds(0, pad)], halo.at[1],
        halo_send.at[1], halo_recv.at[1],
        device_id=(lax.rem(my_e + n_egrp - 1, n_egrp), my_s), device_id_type=MESH,
    )
    next_s = lax.rem(my_s + 1, n_space)
    prev_s = lax.rem(my_s + n_space - 1, n_space)
    up_mob = pltpu.make_async_remote_copy(
        mob_send.at[1], mob_lo, mob_ssem.at[0], mob_rsem.at[0],
        device_id=(my_e, next_s), device_id_type=MESH,
    )
    down_mob = pltpu.make_async_remote_copy(
        mob_send.at[0], mob_hi, mob_ssem.at[1], mob_rsem.at[1],
        device_id=(my_e, prev_s), device_id_type=MESH,
    )

    @pl.when(has_above_e)
    def _():
        up_e.start()

    @pl.when(has_below_e)
    def _():
        down_e.start()

    @pl.when(has_above)
    def _():
        up_mob.start()

    @pl.when(has_below)
    def _():
        down_mob.start()

    for copy in loads:
        copy.wait()

    def residuals(step, accs):
        row = pl.multiple_of(step * STEP, STEP)
        bins = offs[...]
        lam = lam_ref[...]
        energy = my_e * ne + (row + lax.broadcasted_iota(jnp.int32, (STEP, 128), 0)) // rows
        region = tile[...]
        above = None
        for index in range(NREGION):
            shift = bins_ref[index] * rows
            up = even[pl.ds(pad + row + shift, STEP), :]
            down = even[pl.ds(pad + row - shift, STEP), :]
            if above is None:
                above, below = up, down
            else:
                above = jnp.where(region == index, up, above)
                below = jnp.where(region == index, down, below)
        lower = energy - bins
        upper = energy + bins
        dos_low = jnp.where(lower >= 0, dos_of(jnp.maximum(lower, 0)), 0.0)
        dos_high = jnp.where(upper < NE, dos_of(upper), 0.0)
        loss = 1.0 + lam * (1.5 * dos_low + 0.5 * dos_high)
        own_even = even[pl.ds(pad + row, STEP), :]
        own_odd = odd[pl.ds(row, STEP), :]
        gain = lam * dos_of(energy) * (1.5 * above + 0.5 * below)
        res = [
            (own_even + gain) * (1.0 / loss) - own_even,
            own_odd * (1.0 / (loss + lam)) - own_odd,
        ]
        base[0, pl.ds(row, STEP), :] = own_even + 0.5 * res[0]
        base[1, pl.ds(row, STEP), :] = own_odd + 0.5 * res[1]
        new = []
        for field in range(2):
            vectors = [res[field]] + [
                hg[index, field, pl.ds(row, STEP), :].astype(jnp.float32)
                for index in range(HISTORY)
            ]
            for position, (i, j) in enumerate(PAIRS):
                product = vectors[i] * vectors[j]
                new.append(accs[field * len(PAIRS) + position] + (product[:8] + product[8:]))
        return tuple(new)

    accs = tuple(jnp.zeros((8, 128), jnp.float32) for _ in range(2 * len(PAIRS)))
    edge = pad // STEP
    steps = total_rows // STEP
    accs = lax.fori_loop(edge, steps - edge, residuals, accs)

    @pl.when(has_below_e)
    def _():
        up_e.wait_recv()
        even[pl.ds(0, pad), :] = halo[0]

    accs = lax.fori_loop(0, edge, residuals, accs)

    @pl.when(has_above_e)
    def _():
        down_e.wait_recv()
        even[pl.ds(pad + total_rows, pad), :] = halo[1]

    accs = lax.fori_loop(steps - edge, steps, residuals, accs)

    sums[...] = jnp.zeros(sums.shape, jnp.float32)
    for position, acc in enumerate(accs):
        sums[position : position + 1, :] = jnp.sum(acc, axis=0, keepdims=True)
    lane_sum = jnp.sum(sums[...], axis=1, keepdims=True)
    place = lax.broadcasted_iota(jnp.int32, sums.shape, 0) == lax.broadcasted_iota(
        jnp.int32, sums.shape, 1
    )
    row_sum = jnp.sum(jnp.where(place, lane_sum, 0.0), axis=0, keepdims=True)
    part[...] = row_sum
    gathered[me] = row_sum

    def send_sums(step, carry):
        pltpu.make_async_remote_copy(
            part, gathered.at[me], sum_send, sum_recv,
            device_id=device(lax.rem(me + step, count)), device_id_type=MESH,
        ).start()
        return carry

    lax.fori_loop(1, count, send_sums, 0)

    for copy in late:
        copy.wait()

    def join_history(step, carry):
        row = pl.multiple_of(step * STEP, STEP)
        for index in range(HISTORY):
            for field in range(2):
                hist[index, field, pl.ds(row, STEP), :] = hx[
                    index, field, pl.ds(row, STEP), :
                ].astype(jnp.float32) + 0.5 * hg[index, field, pl.ds(row, STEP), :].astype(
                    jnp.float32
                )
        return carry

    lax.fori_loop(0, steps, join_history, 0)

    @pl.when(has_below)
    def _():
        up_mob.wait_recv()

    @pl.when(has_above)
    def _():
        down_mob.wait_recv()

    lanes = lax.broadcasted_iota(jnp.int32, (1, 128), 1)
    column = lanes % COLS
    none = jnp.zeros((1, 128), jnp.float32)
    for row in range(rows):
        mob = mob_ref[row : row + 1, :]
        under = mob_lo[...] if row == 0 else mob_ref[row - 1 : row, :]
        over = mob_hi[...] if row == rows - 1 else mob_ref[row + 1 : row + 2, :]
        w_under = 0.04 * (mob + under)
        w_over = 0.04 * (mob + over)
        if row == 0:
            w_under = jnp.where(has_below, w_under, 0.0)
        if row == rows - 1:
            w_over = jnp.where(has_above, w_over, 0.0)
        w_left = jnp.where(column > 0, 0.04 * (mob + pltpu.roll(mob, 1, 1)), 0.0)
        w_right = jnp.where(column < COLS - 1, 0.04 * (mob + pltpu.roll(mob, 127, 1)), 0.0)
        w_plane = 0.04 * (mob + pltpu.roll(mob, COLS, 1))
        own = 1.0 - (w_under + w_over + w_left + w_right + w_plane)
        parts = (
            own,
            none if row == 0 else w_under,
            none if row == rows - 1 else w_over,
            w_left,
            w_right,
            w_plane,
            w_under if row == 0 else w_over if row == rows - 1 else none,
        )
        for place, value in enumerate(parts):
            for copy_of in range(8 // rows):
                weight[place, copy_of * rows + row : copy_of * rows + row + 1, :] = value

    sums_in = gathered.at[pl.ds(0, count - 1)]
    pltpu.make_async_copy(sums_in, sums_in, sum_recv).wait()
    total = jnp.sum(gathered[...], axis=0)
    coeffs = [
        [jnp.concatenate([c] * (WIDE // 8), axis=0) for c in solve(total, field, used_ref)]
        for field in range(2)
    ]

    piece = ne // PIECES
    blocks = piece * rows // WIDE

    def mix(block, carry):
        row = pl.multiple_of(block * WIDE, WIDE)
        for field in range(2):
            value = coeffs[field][0] * base[field, pl.ds(row, WIDE), :]
            for index in range(HISTORY):
                value = value + coeffs[field][index + 1] * hist[index, field, pl.ds(row, WIDE), :]
            mixed[field, pl.ds(8 + row, WIDE), :] = value
        return carry

    def pack(group, carry):
        first = pl.multiple_of(group * 8, 8)
        for field in range(2):
            for side, row in ((0, 0), (1, rows - 1)):
                packed[side, field, pl.ds(first, 8), :] = mixed[
                    field, pl.ds(8 + first * rows + row, 8, stride=rows), :
                ]
        return carry

    sends = []
    for index in range(PIECES):
        lax.fori_loop(index * blocks, (index + 1) * blocks, mix, 0)
        lax.fori_loop(index * (piece // 8), (index + 1) * (piece // 8), pack, 0)
        span = pl.ds(index * piece, piece)
        up = pltpu.make_async_remote_copy(
            packed.at[1, :, span], lo.at[:, span], edge_send.at[0, index],
            edge_recv.at[0, index], device_id=(my_e, next_s), device_id_type=MESH,
        )
        down = pltpu.make_async_remote_copy(
            packed.at[0, :, span], hi.at[:, span], edge_send.at[1, index],
            edge_recv.at[1, index], device_id=(my_e, prev_s), device_id_type=MESH,
        )
        sends.append((up, down))

        @pl.when(has_above)
        def _():
            up.start()

        @pl.when(has_below)
        def _():
            down.start()

    weights = [weight[place] for place in range(7)]

    def drift(block, carry):
        for part_of in range(WIDE // 8):
            row = pl.multiple_of(block * WIDE + part_of * 8, 8)
            energy = my_e * ne + (row + lax.broadcasted_iota(jnp.int32, (8, 128), 0)) // rows
            drive = 0.25 * dos_of(energy)
            own = [mixed[field, pl.ds(8 + row, 8), :] for field in range(2)]
            for field in range(2):
                value = own[field]
                result = (
                    weights[0] * value
                    + weights[1] * mixed[field, pl.ds(7 + row, 8), :]
                    + weights[2] * mixed[field, pl.ds(9 + row, 8), :]
                    + weights[3] * pltpu.roll(value, 1, 1)
                    + weights[4] * pltpu.roll(value, 127, 1)
                    + weights[5] * pltpu.roll(value, COLS, 1)
                )
                if field == 0:
                    result = result + drive * own[1]
                else:
                    result = result - drive * own[0]
                out[field, pl.ds(row, 8), :] = result
        return carry

    lax.fori_loop(0, PIECES * blocks, drift, 0)

    sublane = lax.broadcasted_iota(jnp.int32, (8, 128), 0)
    places = [
        (sublane < (copy_of * rows + rows // 2), sublane < (copy_of + 1) * rows)
        for copy_of in range(8 // rows)
    ]

    def add_edges(block, carry):
        for part_of in range(WIDE // 8):
            row = pl.multiple_of(block * WIDE + part_of * 8, 8)
            first = block * (WIDE // rows) + part_of * (8 // rows)
            for field in range(2):
                value = None
                for copy_of in reversed(range(8 // rows)):
                    from_hi = hi[field, pl.ds(first + copy_of, 8, stride=0), :]
                    from_lo = lo[field, pl.ds(first + copy_of, 8, stride=0), :]
                    if value is None:
                        value = from_hi
                    else:
                        value = jnp.where(places[copy_of][1], from_hi, value)
                    value = jnp.where(places[copy_of][0], from_lo, value)
                out[field, pl.ds(row, 8), :] = out[field, pl.ds(row, 8), :] + weights[6] * value
        return carry

    for index in range(PIECES):
        up, down = sends[index]

        @pl.when(has_below)
        def _():
            up.wait_recv()

        @pl.when(has_above)
        def _():
            down.wait_recv()

        lax.fori_loop(index * blocks, (index + 1) * blocks, add_edges, 0)

    sums_out = gathered.at[pl.ds(0, count - 1)]
    pltpu.make_async_copy(sums_out, sums_out, sum_send).wait()

    @pl.when(has_above_e)
    def _():
        up_e.wait_send()

    @pl.when(has_below_e)
    def _():
        down_e.wait_send()

    @pl.when(has_above)
    def _():
        up_mob.wait_send()
        for up, _ in sends:
            up.wait_send()

    @pl.when(has_below)
    def _():
        down_mob.wait_send()
        for _, down in sends:
            down.wait_send()


def local(n_egrp, n_space, dist, hist_x, hist_g, mobility, region, phonon_bins, coupling, hist_used):
    ne, rows = dist.shape[1], dist.shape[2]
    total = ne * rows
    pad = KMAX * rows
    count = n_egrp * n_space
    f32 = jnp.float32
    vmem = pl.BlockSpec(memory_space=pltpu.VMEM)
    hbm = pl.BlockSpec(memory_space=pltpu.HBM)
    result = pl.pallas_call(
        functools.partial(kernel, n_egrp, n_space, ne, rows),
        out_shape=jax.ShapeDtypeStruct((2, total, 128), f32),
        in_specs=[hbm] * 8,
        out_specs=vmem,
        scratch_shapes=[
            pltpu.SMEM((NREGION,), jnp.int32),
            pltpu.SMEM((NREGION,), f32),
            pltpu.SMEM((2, HISTORY), jnp.int32),
            pltpu.VMEM((rows, 128), f32),
            pltpu.VMEM((rows, 128), jnp.int32),
            pltpu.VMEM((total + 2 * pad, 128), f32),
            pltpu.VMEM((total, 128), f32),
            pltpu.VMEM((HISTORY, 2, total, 128), jnp.bfloat16),
            pltpu.VMEM((HISTORY, 2, total, 128), jnp.bfloat16),
            pltpu.VMEM((2, total, 128), f32),
            pltpu.VMEM((HISTORY, 2, total, 128), f32),
            pltpu.VMEM((2, total + 16, 128), f32),
            pltpu.VMEM((2, 2, ne, 128), f32),
            pltpu.VMEM((2, ne, 128), f32),
            pltpu.VMEM((2, ne, 128), f32),
            pltpu.VMEM((STEP, 128), jnp.int32),
            pltpu.VMEM((STEP, 128), f32),
            pltpu.VMEM((STEP, 128), jnp.int32),
            pltpu.VMEM((7, 8, 128), f32),
            pltpu.VMEM((2, 1, 128), f32),
            pltpu.VMEM((1, 128), f32),
            pltpu.VMEM((1, 128), f32),
            pltpu.VMEM((32, 128), f32),
            pltpu.VMEM((1, 128), f32),
            pltpu.VMEM((count, 1, 128), f32),
            pltpu.VMEM((2, pad, 128), f32),
            pltpu.SemaphoreType.DMA((2 + 2 * HISTORY,)),
            pltpu.SemaphoreType.DMA((5,)),
            pltpu.SemaphoreType.DMA((2,)),
            pltpu.SemaphoreType.DMA((2,)),
            pltpu.SemaphoreType.DMA((2,)),
            pltpu.SemaphoreType.DMA((2,)),
            pltpu.SemaphoreType.DMA,
            pltpu.SemaphoreType.DMA,
            pltpu.SemaphoreType.DMA((2, PIECES)),
            pltpu.SemaphoreType.DMA((2, PIECES)),
        ],
        compiler_params=pltpu.CompilerParams(
            collective_id=0, has_side_effects=True, vmem_limit_bytes=40 << 20
        ),
    )(
        *[pltpu.with_memory_space_constraint(x, pltpu.HBM) for x in (phonon_bins, coupling, hist_used, mobility, region,
        dist.reshape(2, total, 128),
        hist_x.reshape(HISTORY, 2, total, 128),
        hist_g.reshape(HISTORY, 2, total, 128))],
    )
    return result.reshape(dist.shape)


def solution(mesh):
    in_specs = (
        P(None, "egrp", "space", None),
        P(None, None, "egrp", "space", None),
        P(None, None, "egrp", "space", None),
        P("space", None),
        P("space", None),
        P(),
        P(),
        P(),
    )
    out_specs = P(None, "egrp", "space", None)
    body = functools.partial(local, mesh.shape["egrp"], mesh.shape["space"])
    return jax.shard_map(body, mesh=mesh, in_specs=in_specs, out_specs=out_specs, check_vma=False)
```

```python
import functools
import jax
import jax.numpy as jnp
from jax import lax
from jax.experimental import pallas as pl
from jax.experimental.pallas import tpu as pltpu
from jax.sharding import PartitionSpec as P

NE = 1024
HISTORY = 4
NREGION = 4
KMAX = 64
COLS = 64
PIECES = 4
STEP = 32
WIDE = 32
PAIRS = [(i, j) for i in range(HISTORY + 1) for j in range(i, HISTORY + 1)]
MESH = pl.DeviceIdType.MESH


def dos_of(energy):
    value = (energy.astype(jnp.float32) + 0.5) * (1.0 / NE)
    return value * lax.rsqrt(value)


def solve(total, field, used_ref):
    def entry(i, j):
        lane = field * len(PAIRS) + PAIRS.index((min(i, j), max(i, j)))
        return jnp.broadcast_to(total[:, lane : lane + 1], (8, 128))

    size = HISTORY + 1
    valid = [jnp.ones((8, 128), jnp.float32)]
    for index in range(HISTORY):
        valid.append(jnp.full((8, 128), used_ref[field, index].astype(jnp.float32)))
    first = entry(0, 0)
    low = [[None] * size for _ in range(size)]
    scaled = [[None] * size for _ in range(size)]
    inverse = [None] * size
    for j in range(size):
        for i in range(j, size):
            value = valid[i] * valid[j] * entry(i, j)
            if i == j:
                value = value + (1.0 - valid[i]) * first
            for k in range(j):
                value = value - scaled[i][k] * low[j][k]
            scaled[i][j] = value
        inverse[j] = 1.0 / scaled[j][j]
        for i in range(j + 1, size):
            low[i][j] = scaled[i][j] * inverse[j]
    forward = []
    for i in range(size):
        value = valid[i]
        for k in range(i):
            value = value - low[i][k] * forward[k]
        forward.append(value)
    weights = [None] * size
    for i in reversed(range(size)):
        value = forward[i] * inverse[i]
        for k in range(i + 1, size):
            value = value - low[k][i] * weights[k]
        weights[i] = value
    inv_sum = 1.0 / functools.reduce(lambda a, b: a + b, weights)
    return [w * inv_sum for w in weights]


def kernel(
    n_egrp, n_space, ne, rows,
    bins_hbm, coup_hbm, used_hbm, mob_hbm, region_hbm, dist_hbm, hx_hbm, hg_hbm,
    out,
    bins_ref, coup_ref, used_ref, mob_ref, region_ref,
    even, odd, hg, hx, base, hist, mixed, packed, lo, hi, offs, lam_ref, tile, weight,
    mob_send, mob_lo, mob_hi, sums, part, gathered, halo,
    in_sem, small_sem, halo_send, halo_recv, mob_ssem, mob_rsem, sum_send, sum_recv,
    edge_send, edge_recv,
):
    my_e = lax.axis_index("egrp")
    my_s = lax.axis_index("space")
    count = n_egrp * n_space
    me = my_e * n_space + my_s
    total_rows = ne * rows
    pad = KMAX * rows

    def device(index):
        return (index // n_space, lax.rem(index, n_space))

    small = [
        pltpu.make_async_copy(source, target, small_sem.at[index])
        for index, (source, target) in enumerate((
            (region_hbm, region_ref), (bins_hbm, bins_ref), (coup_hbm, coup_ref),
            (mob_hbm, mob_ref), (used_hbm, used_ref),
        ))
    ]
    loads = [
        pltpu.make_async_copy(dist_hbm.at[0], even.at[pl.ds(pad, total_rows)], in_sem.at[0]),
        pltpu.make_async_copy(dist_hbm.at[1], odd, in_sem.at[1]),
    ]
    for index in range(HISTORY):
        loads.append(pltpu.make_async_copy(hg_hbm.at[index], hg.at[index], in_sem.at[2 + index]))
    late = [
        pltpu.make_async_copy(hx_hbm.at[index], hx.at[index], in_sem.at[2 + HISTORY + index])
        for index in range(HISTORY)
    ]
    for copy in small + loads + late:
        copy.start()

    barrier = pltpu.get_barrier_semaphore()

    def greet(step, carry):
        pl.semaphore_signal(
            barrier, inc=1, device_id=device(lax.rem(me + step, count)), device_id_type=MESH
        )
        return carry

    lax.fori_loop(1, count, greet, 0)

    for copy in small:
        copy.wait()
    for copy_of in range(STEP // rows):
        tile[pl.ds(copy_of * rows, rows), :] = region_ref[...]
    region = tile[...]
    inside = [region == index for index in range(NREGION)]
    bins = jnp.zeros((STEP, 128), jnp.int32)
    lam = jnp.zeros((STEP, 128), jnp.float32)
    for index in range(NREGION):
        bins = jnp.where(inside[index], bins_ref[index], bins)
        lam = jnp.where(inside[index], coup_ref[index], lam)
    offs[...] = bins
    lam_ref[...] = lam
    mob_send[0] = mob_ref[0:1, :]
    mob_send[1] = mob_ref[rows - 1 : rows, :]

    has_below_e = my_e > 0
    has_above_e = my_e < n_egrp - 1
    has_below = my_s > 0
    has_above = my_s < n_space - 1

    for field in range(2):
        mixed[field, pl.ds(0, 8), :] = jnp.zeros((8, 128), jnp.float32)
        mixed[field, pl.ds(8 + total_rows, 8), :] = jnp.zeros((8, 128), jnp.float32)
    even[pl.ds(0, pad), :] = jnp.zeros((pad, 128), jnp.float32)
    even[pl.ds(pad + total_rows, pad), :] = jnp.zeros((pad, 128), jnp.float32)

    @pl.when(my_s == 0)
    def _():
        lo[...] = jnp.zeros(lo.shape, jnp.float32)
        mob_lo[...] = jnp.zeros(mob_lo.shape, jnp.float32)

    @pl.when(my_s == n_space - 1)
    def _():
        hi[...] = jnp.zeros(hi.shape, jnp.float32)
        mob_hi[...] = jnp.zeros(mob_hi.shape, jnp.float32)

    pl.semaphore_wait(barrier, count - 1)

    up_e = pltpu.make_async_remote_copy(
        dist_hbm.at[0, pl.ds(total_rows - pad, pad)], halo.at[0],
        halo_send.at[0], halo_recv.at[0],
        device_id=(lax.rem(my_e + 1, n_egrp), my_s), device_id_type=MESH,
    )
    down_e = pltpu.make_async_remote_copy(
        dist_hbm.at[0, pl.ds(0, pad)], halo.at[1],
        halo_send.at[1], halo_recv.at[1],
        device_id=(lax.rem(my_e + n_egrp - 1, n_egrp), my_s), device_id_type=MESH,
    )
    next_s = lax.rem(my_s + 1, n_space)
    prev_s = lax.rem(my_s + n_space - 1, n_space)
    up_mob = pltpu.make_async_remote_copy(
        mob_send.at[1], mob_lo, mob_ssem.at[0], mob_rsem.at[0],
        device_id=(my_e, next_s), device_id_type=MESH,
    )
    down_mob = pltpu.make_async_remote_copy(
        mob_send.at[0], mob_hi, mob_ssem.at[1], mob_rsem.at[1],
        device_id=(my_e, prev_s), device_id_type=MESH,
    )

    @pl.when(has_above_e)
    def _():
        up_e.start()

    @pl.when(has_below_e)
    def _():
        down_e.start()

    @pl.when(has_above)
    def _():
        up_mob.start()

    @pl.when(has_below)
    def _():
        down_mob.start()

    for copy in loads:
        copy.wait()

    def residuals(step, accs):
        row = pl.multiple_of(step * STEP, STEP)
        bins = offs[...]
        lam = lam_ref[...]
        energy = my_e * ne + (row + lax.broadcasted_iota(jnp.int32, (STEP, 128), 0)) // rows
        region = tile[...]
        above = None
        for index in range(NREGION):
            shift = bins_ref[index] * rows
            up = even[pl.ds(pad + row + shift, STEP), :]
            down = even[pl.ds(pad + row - shift, STEP), :]
            if above is None:
                above, below = up, down
            else:
                above = jnp.where(region == index, up, above)
                below = jnp.where(region == index, down, below)
        lower = energy - bins
        upper = energy + bins
        dos_low = jnp.where(lower >= 0, dos_of(jnp.maximum(lower, 0)), 0.0)
        dos_high = jnp.where(upper < NE, dos_of(upper), 0.0)
        loss = 1.0 + lam * (1.5 * dos_low + 0.5 * dos_high)
        own_even = even[pl.ds(pad + row, STEP), :]
        own_odd = odd[pl.ds(row, STEP), :]
        both = 1.0 / (loss * (loss + lam))
        gain = lam * dos_of(energy) * (1.5 * above + 0.5 * below)
        res = [
            (own_even + gain) * (both * (loss + lam)) - own_even,
            own_odd * (both * loss) - own_odd,
        ]
        base[0, pl.ds(row, STEP), :] = own_even + 0.5 * res[0]
        base[1, pl.ds(row, STEP), :] = own_odd + 0.5 * res[1]
        new = []
        for field in range(2):
            vectors = [res[field]] + [
                hg[index, field, pl.ds(row, STEP), :].astype(jnp.float32)
                for index in range(HISTORY)
            ]
            for position, (i, j) in enumerate(PAIRS):
                product = vectors[i] * vectors[j]
                new.append(accs[field * len(PAIRS) + position] + jnp.sum(product.reshape(STEP // 8, 8, 128), axis=0))
        return tuple(new)

    accs = tuple(jnp.zeros((8, 128), jnp.float32) for _ in range(2 * len(PAIRS)))
    edge = pad // STEP
    steps = total_rows // STEP
    accs = lax.fori_loop(edge, steps - edge, residuals, accs)

    @pl.when(has_below_e)
    def _():
        up_e.wait_recv()
        even[pl.ds(0, pad), :] = halo[0]

    accs = lax.fori_loop(0, edge, residuals, accs)

    @pl.when(has_above_e)
    def _():
        down_e.wait_recv()
        even[pl.ds(pad + total_rows, pad), :] = halo[1]

    accs = lax.fori_loop(steps - edge, steps, residuals, accs)

    sums[...] = jnp.zeros(sums.shape, jnp.float32)
    for position, acc in enumerate(accs):
        sums[position : position + 1, :] = jnp.sum(acc, axis=0, keepdims=True)
    lane_sum = jnp.sum(sums[...], axis=1, keepdims=True)
    place = lax.broadcasted_iota(jnp.int32, sums.shape, 0) == lax.broadcasted_iota(
        jnp.int32, sums.shape, 1
    )
    row_sum = jnp.sum(jnp.where(place, lane_sum, 0.0), axis=0, keepdims=True)
    part[...] = row_sum
    gathered[me] = row_sum

    def send_sums(step, carry):
        pltpu.make_async_remote_copy(
            part, gathered.at[me], sum_send, sum_recv,
            device_id=device(lax.rem(me + step, count)), device_id_type=MESH,
        ).start()
        return carry

    lax.fori_loop(1, count, send_sums, 0)

    for copy in late:
        copy.wait()

    def join_history(step, carry):
        row = pl.multiple_of(step * STEP, STEP)
        for index in range(HISTORY):
            for field in range(2):
                hist[index, field, pl.ds(row, STEP), :] = hx[
                    index, field, pl.ds(row, STEP), :
                ].astype(jnp.float32) + 0.5 * hg[index, field, pl.ds(row, STEP), :].astype(
                    jnp.float32
                )
        return carry

    lax.fori_loop(0, steps, join_history, 0)

    @pl.when(has_below)
    def _():
        up_mob.wait_recv()

    @pl.when(has_above)
    def _():
        down_mob.wait_recv()

    lanes = lax.broadcasted_iota(jnp.int32, (1, 128), 1)
    column = lanes % COLS
    none = jnp.zeros((1, 128), jnp.float32)
    for row in range(rows):
        mob = mob_ref[row : row + 1, :]
        under = mob_lo[...] if row == 0 else mob_ref[row - 1 : row, :]
        over = mob_hi[...] if row == rows - 1 else mob_ref[row + 1 : row + 2, :]
        w_under = 0.04 * (mob + under)
        w_over = 0.04 * (mob + over)
        if row == 0:
            w_under = jnp.where(has_below, w_under, 0.0)
        if row == rows - 1:
            w_over = jnp.where(has_above, w_over, 0.0)
        w_left = jnp.where(column > 0, 0.04 * (mob + pltpu.roll(mob, 1, 1)), 0.0)
        w_right = jnp.where(column < COLS - 1, 0.04 * (mob + pltpu.roll(mob, 127, 1)), 0.0)
        w_plane = 0.04 * (mob + pltpu.roll(mob, COLS, 1))
        own = 1.0 - (w_under + w_over + w_left + w_right + w_plane)
        parts = (
            own,
            none if row == 0 else w_under,
            none if row == rows - 1 else w_over,
            w_left,
            w_right,
            w_plane,
            w_under if row == 0 else w_over if row == rows - 1 else none,
        )
        for place, value in enumerate(parts):
            for copy_of in range(8 // rows):
                weight[place, copy_of * rows + row : copy_of * rows + row + 1, :] = value

    sums_in = gathered.at[pl.ds(0, count - 1)]
    pltpu.make_async_copy(sums_in, sums_in, sum_recv).wait()
    total = jnp.sum(gathered[...], axis=0)
    coeffs = [
        [jnp.concatenate([c] * (WIDE // 8), axis=0) for c in solve(total, field, used_ref)]
        for field in range(2)
    ]

    piece = ne // PIECES
    blocks = piece * rows // WIDE

    def mix(block, carry):
        row = pl.multiple_of(block * WIDE, WIDE)
        for field in range(2):
            value = coeffs[field][0] * base[field, pl.ds(row, WIDE), :]
            for index in range(HISTORY):
                value = value + coeffs[field][index + 1] * hist[index, field, pl.ds(row, WIDE), :]
            mixed[field, pl.ds(8 + row, WIDE), :] = value
        return carry

    def pack(group, carry):
        first = pl.multiple_of(group * 8, 8)
        for field in range(2):
            for side, row in ((0, 0), (1, rows - 1)):
                packed[side, field, pl.ds(first, 8), :] = mixed[
                    field, pl.ds(8 + first * rows + row, 8, stride=rows), :
                ]
        return carry

    sends = []
    for index in range(PIECES):
        lax.fori_loop(index * blocks, (index + 1) * blocks, mix, 0)
        lax.fori_loop(index * (piece // 8), (index + 1) * (piece // 8), pack, 0)
        span = pl.ds(index * piece, piece)
        up = pltpu.make_async_remote_copy(
            packed.at[1, :, span], lo.at[:, span], edge_send.at[0, index],
            edge_recv.at[0, index], device_id=(my_e, next_s), device_id_type=MESH,
        )
        down = pltpu.make_async_remote_copy(
            packed.at[0, :, span], hi.at[:, span], edge_send.at[1, index],
            edge_recv.at[1, index], device_id=(my_e, prev_s), device_id_type=MESH,
        )
        sends.append((up, down))

        @pl.when(has_above)
        def _():
            up.start()

        @pl.when(has_below)
        def _():
            down.start()

    weights = [weight[place] for place in range(7)]

    def drift(block, carry):
        for part_of in range(WIDE // 8):
            row = pl.multiple_of(block * WIDE + part_of * 8, 8)
            energy = my_e * ne + (row + lax.broadcasted_iota(jnp.int32, (8, 128), 0)) // rows
            drive = 0.25 * dos_of(energy)
            own = [mixed[field, pl.ds(8 + row, 8), :] for field in range(2)]
            for field in range(2):
                value = own[field]
                result = (
                    weights[0] * value
                    + weights[1] * mixed[field, pl.ds(7 + row, 8), :]
                    + weights[2] * mixed[field, pl.ds(9 + row, 8), :]
                    + weights[3] * pltpu.roll(value, 1, 1)
                    + weights[4] * pltpu.roll(value, 127, 1)
                    + weights[5] * pltpu.roll(value, COLS, 1)
                )
                if field == 0:
                    result = result + drive * own[1]
                else:
                    result = result - drive * own[0]
                out[field, pl.ds(row, 8), :] = result
        return carry

    lax.fori_loop(0, PIECES * blocks, drift, 0)

    sublane = lax.broadcasted_iota(jnp.int32, (8, 128), 0)
    places = [
        (sublane < (copy_of * rows + rows // 2), sublane < (copy_of + 1) * rows)
        for copy_of in range(8 // rows)
    ]

    def add_edges(block, carry):
        for part_of in range(WIDE // 8):
            row = pl.multiple_of(block * WIDE + part_of * 8, 8)
            first = block * (WIDE // rows) + part_of * (8 // rows)
            for field in range(2):
                value = None
                for copy_of in reversed(range(8 // rows)):
                    from_hi = hi[field, pl.ds(first + copy_of, 8, stride=0), :]
                    from_lo = lo[field, pl.ds(first + copy_of, 8, stride=0), :]
                    if value is None:
                        value = from_hi
                    else:
                        value = jnp.where(places[copy_of][1], from_hi, value)
                    value = jnp.where(places[copy_of][0], from_lo, value)
                out[field, pl.ds(row, 8), :] = out[field, pl.ds(row, 8), :] + weights[6] * value
        return carry

    for index in range(PIECES):
        up, down = sends[index]

        @pl.when(has_below)
        def _():
            up.wait_recv()

        @pl.when(has_above)
        def _():
            down.wait_recv()

        lax.fori_loop(index * blocks, (index + 1) * blocks, add_edges, 0)

    sums_out = gathered.at[pl.ds(0, count - 1)]
    pltpu.make_async_copy(sums_out, sums_out, sum_send).wait()

    @pl.when(has_above_e)
    def _():
        up_e.wait_send()

    @pl.when(has_below_e)
    def _():
        down_e.wait_send()

    @pl.when(has_above)
    def _():
        up_mob.wait_send()
        for up, _ in sends:
            up.wait_send()

    @pl.when(has_below)
    def _():
        down_mob.wait_send()
        for _, down in sends:
            down.wait_send()


def local(n_egrp, n_space, dist, hist_x, hist_g, mobility, region, phonon_bins, coupling, hist_used):
    ne, rows = dist.shape[1], dist.shape[2]
    total = ne * rows
    pad = KMAX * rows
    count = n_egrp * n_space
    f32 = jnp.float32
    vmem = pl.BlockSpec(memory_space=pltpu.VMEM)
    hbm = pl.BlockSpec(memory_space=pltpu.HBM)
    result = pl.pallas_call(
        functools.partial(kernel, n_egrp, n_space, ne, rows),
        out_shape=jax.ShapeDtypeStruct((2, total, 128), f32),
        in_specs=[hbm] * 8,
        out_specs=vmem,
        scratch_shapes=[
            pltpu.SMEM((NREGION,), jnp.int32),
            pltpu.SMEM((NREGION,), f32),
            pltpu.SMEM((2, HISTORY), jnp.int32),
            pltpu.VMEM((rows, 128), f32),
            pltpu.VMEM((rows, 128), jnp.int32),
            pltpu.VMEM((total + 2 * pad, 128), f32),
            pltpu.VMEM((total, 128), f32),
            pltpu.VMEM((HISTORY, 2, total, 128), jnp.bfloat16),
            pltpu.VMEM((HISTORY, 2, total, 128), jnp.bfloat16),
            pltpu.VMEM((2, total, 128), f32),
            pltpu.VMEM((HISTORY, 2, total, 128), f32),
            pltpu.VMEM((2, total + 16, 128), f32),
            pltpu.VMEM((2, 2, ne, 128), f32),
            pltpu.VMEM((2, ne, 128), f32),
            pltpu.VMEM((2, ne, 128), f32),
            pltpu.VMEM((STEP, 128), jnp.int32),
            pltpu.VMEM((STEP, 128), f32),
            pltpu.VMEM((STEP, 128), jnp.int32),
            pltpu.VMEM((7, 8, 128), f32),
            pltpu.VMEM((2, 1, 128), f32),
            pltpu.VMEM((1, 128), f32),
            pltpu.VMEM((1, 128), f32),
            pltpu.VMEM((32, 128), f32),
            pltpu.VMEM((1, 128), f32),
            pltpu.VMEM((count, 1, 128), f32),
            pltpu.VMEM((2, pad, 128), f32),
            pltpu.SemaphoreType.DMA((2 + 2 * HISTORY,)),
            pltpu.SemaphoreType.DMA((5,)),
            pltpu.SemaphoreType.DMA((2,)),
            pltpu.SemaphoreType.DMA((2,)),
            pltpu.SemaphoreType.DMA((2,)),
            pltpu.SemaphoreType.DMA((2,)),
            pltpu.SemaphoreType.DMA,
            pltpu.SemaphoreType.DMA,
            pltpu.SemaphoreType.DMA((2, PIECES)),
            pltpu.SemaphoreType.DMA((2, PIECES)),
        ],
        compiler_params=pltpu.CompilerParams(
            collective_id=0, has_side_effects=True, vmem_limit_bytes=40 << 20
        ),
    )(
        *[pltpu.with_memory_space_constraint(x, pltpu.HBM) for x in (phonon_bins, coupling, hist_used, mobility, region,
        dist.reshape(2, total, 128),
        hist_x.reshape(HISTORY, 2, total, 128),
        hist_g.reshape(HISTORY, 2, total, 128))],
    )
    return result.reshape(dist.shape)


def solution(mesh):
    in_specs = (
        P(None, "egrp", "space", None),
        P(None, None, "egrp", "space", None),
        P(None, None, "egrp", "space", None),
        P("space", None),
        P("space", None),
        P(),
        P(),
        P(),
    )
    out_specs = P(None, "egrp", "space", None)
    body = functools.partial(local, mesh.shape["egrp"], mesh.shape["space"])
    return jax.shard_map(body, mesh=mesh, in_specs=in_specs, out_specs=out_specs, check_vma=False)
```
